128 devices in a mesh: gx: 4 (over x), gy: 4 (over z), gz: 8 (over y, core).
Axes of the slice: x: 4, y: 4, z: 4, core: 2. Of those that a mesh axis runs over, the one named last changes fastest.
Arguments:
- state: float32 [16, 32, 256, 256], P('gx', 'gy', 'gz'), may hold values from -6 to 6
- convection: bfloat16 [16, 32, 256, 4096], P('gx', 'gy', 'gz'), may hold values from -0.375 to 0.375
- inverse_mass: bfloat16 [16, 32, 256, 4096], P('gx', 'gy', 'gz'), may hold values from -0.75 to 0.75
- face_coupling: bfloat16 [96, 64], replicated, may hold values from -0.3125 to 0.3125
- lower_bound: float32 [16, 32, 256, 256], P('gx', 'gy', 'gz'), may hold values from -3 to -1
- upper_bound: float32 [16, 32, 256, 256], P('gx', 'gy', 'gz'), may hold values from 1 to 3
- new_owner: int32 [128, 1024, 1], P(('gx', 'gy', 'gz')), may hold values from 0 to 127; in each aligned block of 1024 rows (0 to 1023, 1024 to 2047, ..., all dimensions but the last counted through in order) at most 16 rows name the same one
Outputs:
- handed: float32 [262144, 256], P(('gx', 'gy', 'gz'))
The draws below stay inside these ranges and needn't reach their ends.
Inputs may be any that keep to these rules, and one draw needn't show every extreme that they name: `new_owner`: among the zones of one device no owner is named more than 16 times, a bound that some block reaches.
All inputs are finite; a program needn't handle non-finite values.
Results may differ from the reference program's by a relative error of at most 0.003.
Values may be sent and summed in bfloat16 or wider, within the bound.
No kernel may reach another device: no remote copies, remote signals or barrier semaphores. Data moves between devices by JAX's collectives and lax.ppermute only.
A program may use at most 128 MiB of HBM per device.

```python
import math
import jax
import jax.numpy as jnp
import numpy as np
from jax import lax

COMP = 4
DOFS = 64
STEPS = 2
EX = 4
EY = 8
EZ = 32
ZONES_DEV = 1024
CAP = 16
NX = 16
NY = 32
NZ = 256
N_GX = 4
N_GY = 4
N_GZ = 8
DEVICES = 128


def levels(key, extent, split, low, high):
    level = 1.0
    for position, parts in split:
        heights = jax.random.uniform(jax.random.fold_in(jax.random.fold_in(key, 6), position), (parts,), jnp.float32, low / len(split), high / len(split))
        level = level * jnp.repeat(jnp.exp(heights), extent[position] // parts).reshape((-1,) + (1,) * (len(extent) - 1 - position))
    return level


def shared_out(key, own, number, rows, count, top, reach, slope):
    order = jax.random.permutation(key, count)
    heavy_load, common = shares(count, rows * top, reach, slope, True), shares(count, rows * top, reach, slope, False)
    places = jnp.arange(count)

    def named(sizes, turn):
        used = int((sizes > 0).sum())
        fixed = max(1, used // 4)
        moved = fixed + (places - fixed + turn * (used - fixed)) % max(1, count - fixed)
        return jnp.zeros((count,), jnp.int32).at[order[jnp.where(places < fixed, places, moved)]].set(jnp.asarray(sizes, jnp.int32))

    sizes = jnp.where(number % 4 == 0, named(heavy_load, number // 4), named(common, number - number // 4 - 1))
    mixed = jax.random.permutation(jax.random.fold_in(own, 3), count)
    giver, taker = mixed[0:count // 2 * 2:2], mixed[1:count // 2 * 2:2]
    room = jnp.minimum(sizes[giver] - 1, reach - sizes[taker]) // 2
    room = jnp.where((giver == order[0]) | (taker == order[0]) | (sizes[taker] == 0), 0, jnp.maximum(room, 0))
    moved = jax.random.randint(jax.random.fold_in(own, 4), (count // 2,), 0, 1 << 20) % (room + 1)
    sizes = sizes.at[giver].add(-moved).at[taker].add(moved)
    members = jnp.searchsorted(jnp.cumsum(sizes), jnp.arange(rows * top), side="right").astype(jnp.int32)
    grid = members.reshape(top, rows).T
    grid = grid[jax.random.permutation(jax.random.fold_in(own, 1), rows)]
    turn = jax.random.randint(jax.random.fold_in(own, 2), (rows, 1), 0, top)
    return jnp.take_along_axis(grid, (jnp.arange(top)[None, :] + turn) % top, axis=1)


def shares(number_of, total, reach, slope, full):
    loads = [(1 << 20) // math.isqrt(rank ** slope) + 1 for rank in range(1, number_of + 1)]
    largest = reach if full else min(reach, max(-(-total // number_of), total * loads[0] // sum(loads)))
    least = 1 if total - largest >= number_of - 1 else 0
    holding, rest = [largest] + [least] * (number_of - 1), total - largest - least * (number_of - 1)
    while rest > 0:
        free = [i for i in range(1, number_of) if holding[i] < largest] or [i for i in range(1, number_of) if holding[i] < reach]
        mass, remaining = sum([loads[i] for i in free]), rest
        for i in free:
            addition = min(reach - holding[i], max(1, remaining * loads[i] // mass), rest)
            holding[i] = holding[i] + addition
            rest = rest - addition
    return np.array(holding)


def noise(rng, extent, scale, most, shards=(), kind=jnp.bfloat16):
    result = scale * jax.random.normal(rng, extent, jnp.float32)
    if shards:
        result = result * levels(rng, extent, shards, -0.22, 0.18)
    return jnp.clip(result, -most, most).astype(kind)


def setup_inputs(seed: int = 0) -> dict:
    streams_of = jax.random.split(jax.random.key(seed), 8)
    state = noise(streams_of[0], (NX, NY, NZ, COMP * DOFS), 1.0, 6.0, ((0, 4), (1, 4), (2, 8)), jnp.float32)
    convection = noise(streams_of[1], (NX, NY, NZ, DOFS * DOFS), (4 * DOFS) ** -0.5, 0.375, ((0, 4), (1, 4), (2, 8)))
    inverse_mass = noise(streams_of[2], (NX, NY, NZ, DOFS * DOFS), DOFS ** -0.5, 0.75, ((0, 4), (1, 4), (2, 8)))
    face_coupling = noise(streams_of[3], (96, DOFS), 384 ** -0.5, 0.3125)
    lower_bound = jnp.clip(-3.0 + 2.0 * jax.random.uniform(streams_of[4], (NX, NY, NZ, COMP * DOFS), jnp.float32) ** levels(streams_of[4], (NX, NY, NZ, COMP * DOFS), ((0, 4), (1, 4), (2, 8)), -0.2, 0.2), -3.0, -1.0)
    upper_bound = jnp.clip(1.0 + 2.0 * jax.random.uniform(streams_of[5], (NX, NY, NZ, COMP * DOFS), jnp.float32) ** levels(streams_of[5], (NX, NY, NZ, COMP * DOFS), ((0, 4), (1, 4), (2, 8)), -0.2, 0.2), 1.0, 3.0)
    new_owner_keys = jax.random.split(jax.random.fold_in(streams_of[6], 1), DEVICES * ZONES_DEV // ZONES_DEV)
    new_owner_turns = jax.random.permutation(jax.random.fold_in(streams_of[6], 3), DEVICES * ZONES_DEV // ZONES_DEV)
    new_owner = jax.vmap(lambda own, number: shared_out(jax.random.fold_in(streams_of[6], 2), own, number, ZONES_DEV, DEVICES, 1, CAP, 2))(new_owner_keys, new_owner_turns).reshape((DEVICES, ZONES_DEV, 1))
    return dict(state=state, convection=convection, inverse_mass=inverse_mass, face_coupling=face_coupling, lower_bound=lower_bound, upper_bound=upper_bound, new_owner=new_owner)


HIGH = lax.Precision.HIGHEST


def neighbour(face, axis, lower):
    count = face.shape[axis]
    widths = [(0, 0)] * face.ndim
    if lower:
        widths[axis] = (1, 0)
        return lax.slice_in_dim(jnp.pad(face, widths), 0, count, axis=axis)
    widths[axis] = (0, 1)
    return lax.slice_in_dim(jnp.pad(face, widths), 1, count + 1, axis=axis)


def remap(state, convection, inverse_mass, face_coupling, lower_bound, upper_bound):
    nx, ny, nz = state.shape[0], state.shape[1], state.shape[2]
    work = state.astype(jnp.bfloat16)
    cube = work.reshape(nx, ny, nz, COMP, 4, 4, 4)

    def flat(face):
        return face.reshape(nx, ny, nz, COMP, 16)

    incoming = jnp.concatenate([
        neighbour(flat(cube[:, :, :, :, 3, :, :]), 0, True),
        neighbour(flat(cube[:, :, :, :, 0, :, :]), 0, False),
        neighbour(flat(cube[:, :, :, :, :, 3, :]), 1, True),
        neighbour(flat(cube[:, :, :, :, :, 0, :]), 1, False),
        neighbour(flat(cube[:, :, :, :, :, :, 3]), 2, True),
        neighbour(flat(cube[:, :, :, :, :, :, 0]), 2, False)], axis=-1)
    flux = jnp.einsum("xyzcf,fi->xyzci", incoming.astype(jnp.float32), face_coupling.astype(jnp.float32), precision=HIGH)

    def slab(pieces):
        conv, inverse, worked, flowing, current, lower, upper = pieces
        conv = conv.astype(jnp.float32).reshape(ny, nz, DOFS, DOFS)
        inverse = inverse.astype(jnp.float32).reshape(ny, nz, DOFS, DOFS)
        values = worked.astype(jnp.float32).reshape(ny, nz, COMP, DOFS)
        pushed = jnp.einsum("yzij,yzcj->yzci", conv, values, precision=HIGH)
        rhs = (pushed + flowing).astype(jnp.bfloat16)
        rhs = lax.optimization_barrier(rhs).astype(jnp.float32)
        change = jnp.einsum("yzij,yzcj->yzci", inverse, rhs, precision=HIGH)
        moved = current + change.reshape(ny, nz, COMP * DOFS)
        return jnp.minimum(jnp.maximum(moved, lower), upper)

    return lax.map(slab, (convection, inverse_mass, work, flux, state, lower_bound, upper_bound))


def reference(state, convection, inverse_mass, face_coupling, lower_bound, upper_bound, new_owner):
    for step in range(STEPS):
        state = remap(state, convection, inverse_mass, face_coupling, lower_bound, upper_bound)
    devices = N_GX * N_GY * N_GZ
    width = COMP * DOFS
    blocks = state.reshape(N_GX, EX, N_GY, EY, N_GZ, EZ, width)
    blocks = blocks.transpose(0, 2, 4, 1, 3, 5, 6).reshape(devices, EX * EY * EZ, width)
    owner = new_owner[:, :, 0].astype(jnp.int32)
    onehot = (owner[:, :, None] == jnp.arange(devices, dtype=jnp.int32)[None, None, :]).astype(jnp.int32)
    running = jnp.cumsum(onehot, axis=1).astype(jnp.int32)
    rank = (jnp.sum(running * onehot, axis=2) - 1).astype(jnp.int32)
    slot = (owner * CAP + rank).astype(jnp.int32)

    def place(target, rows):
        return jnp.zeros((devices * CAP, width), rows.dtype).at[target].set(rows)

    sent = jax.vmap(place)(slot, blocks)
    return sent.reshape(devices, devices, CAP, width).transpose(1, 0, 2, 3).reshape(devices * devices * CAP, width)
```

```python
import jax
import jax.numpy as jnp
import numpy as np
from jax import lax
from jax.experimental import pallas as pl
from jax.experimental.pallas import tpu as pltpu
from jax.sharding import PartitionSpec as P

COMP = 4
DOFS = 64
STEPS = 2
WIDTH = COMP * DOFS
EX, EY, EZ = 4, 8, 32
ZONES = EX * EY * EZ
PLANE = EY * EZ
TILE = 128
TILES = ZONES // TILE
ROWS = 8
FACE = COMP * 16
CAP = 16
AXES = ("gx", "gy", "gz")
F32 = jnp.float32
BF16 = jnp.bfloat16


def pick_table():
    table = np.zeros((6, COMP, 16, COMP, 4, 4, 4), np.float32)
    for c in range(COMP):
        for f in range(16):
            p, q = f // 4, f % 4
            for side, level in ((0, 3), (1, 0)):
                table[0 + side, c, f, c, level, p, q] = 1
                table[2 + side, c, f, c, p, level, q] = 1
                table[4 + side, c, f, c, p, q, level] = 1
    return table.reshape(6 * FACE, WIDTH)


def dot(a, b):
    return jnp.dot(a, b, preferred_element_type=F32)


def select_zones(zone_of, count):
    column = lax.broadcasted_iota(jnp.int32, (1, 128), 1)
    wanted = jnp.where(column < count, zone_of(column), -1)
    zone = lax.broadcasted_iota(jnp.int32, (ZONES, 128), 0)
    return jnp.where(zone == wanted, 1.0, 0.0).astype(BF16)


def place_zones(zone_of, count):
    row = lax.broadcasted_iota(jnp.int32, (128, 1), 0)
    wanted = jnp.where(row < count, zone_of(row), -1)
    zone = lax.broadcasted_iota(jnp.int32, (128, ZONES), 1)
    return jnp.where(zone == wanted, 1.0, 0.0).astype(BF16)


def y_zone(level):
    return lambda n: (n // EZ) * PLANE + level * EZ + n % EZ


def z_zone(level):
    return lambda n: n * EZ + level


SENDS = ((64, 256), (64, 256), (64, 128), (64, 128), (64, 128), (64, 128))


def write_faces(work, pick_ref, flags_ref, payload_ref, send_refs):
    payload = dot(pick_ref[...], work).astype(BF16)
    payload_ref[...] = payload

    def face(k):
        return payload[FACE * k : FACE * (k + 1)]

    pieces = (
        face(0)[:, ZONES - PLANE :].astype(F32),
        face(1)[:, :PLANE].astype(F32),
        dot(face(2), select_zones(y_zone(EY - 1), EX * EZ)),
        dot(face(3), select_zones(y_zone(0), EX * EZ)),
        dot(face(4), select_zones(z_zone(EZ - 1), EX * EY)),
        dot(face(5), select_zones(z_zone(0), EX * EY)),
    )
    for k in range(6):
        send_refs[k][...] = jnp.where(flags_ref[k] > 0, pieces[k], 0.0).astype(BF16)


def incoming_flux(payload_ref, halo_refs, spread_ref, incoming_ref, flux_ref):
    def face(k):
        return payload_ref[FACE * k : FACE * (k + 1), :]

    incoming_ref[0:FACE, 0:PLANE] = halo_refs[0][...]
    incoming_ref[0:FACE, PLANE:ZONES] = payload_ref[0:FACE, 0 : ZONES - PLANE]
    incoming_ref[FACE : 2 * FACE, 0 : ZONES - PLANE] = payload_ref[FACE : 2 * FACE, PLANE:ZONES]
    incoming_ref[FACE : 2 * FACE, ZONES - PLANE : ZONES] = halo_refs[1][...]
    zone = lax.broadcasted_iota(jnp.int32, (FACE, ZONES), 1)
    third = zone % EZ
    second = zone // EZ % EY
    cases = (
        (2, EZ, second == 0, y_zone(0), EX * EZ),
        (3, ZONES - EZ, second == EY - 1, y_zone(EY - 1), EX * EZ),
        (4, 1, third == 0, z_zone(0), EX * EY),
        (5, ZONES - 1, third == EZ - 1, z_zone(EZ - 1), EX * EY),
    )
    for k, shift, edge, zone_of, count in cases:
        moved = pltpu.roll(face(k).astype(F32), shift, 1)
        placed = dot(halo_refs[k][...], place_zones(zone_of, count))
        incoming_ref[FACE * k : FACE * (k + 1), :] = jnp.where(edge, placed, moved).astype(BF16)
    flux_ref[...] = dot(spread_ref[...], incoming_ref[...])


def fold(parts):
    row = lax.broadcasted_iota(jnp.int32, (8, TILE), 0)
    for half in (4, 2, 1):
        low = (row & half) == 0
        count = len(parts) // 2
        joined = []
        for n in range(count):
            a, b = parts[n], parts[n + count]
            x = jnp.where(low, a, b)
            y = jnp.where(low, b, a)
            if half == 4:
                joined.append(x + pltpu.roll(y, 4, 0))
            else:
                joined.append(x + jnp.where(low, pltpu.roll(y, 8 - half, 0), pltpu.roll(y, half, 0)))
        parts = joined
    return parts[0]


def apply_matrices(matrix_ref, values, out_ref):
    comps = [values[DOFS * c : DOFS * (c + 1)] for c in range(COMP)]

    def rows(block, carry):
        start = pl.multiple_of(block * (ROWS * DOFS), ROWS * DOFS)
        parts = [[None] * ROWS for _ in range(COMP)]
        for pair in range(ROWS // 2):
            piece = matrix_ref[:, pl.ds(start + pair * TILE, TILE)].T.astype(F32)
            for half in range(2):
                entry = piece[DOFS * half : DOFS * (half + 1)]
                for c in range(COMP):
                    product = entry * comps[c]
                    total = product[0:8]
                    for k in range(1, 8):
                        total = total + product[8 * k : 8 * k + 8]
                    parts[c][2 * pair + half] = total
        for c in range(COMP):
            out_ref[pl.ds(pl.multiple_of(c * DOFS + block * ROWS, ROWS), ROWS), :] = fold(parts[c])
        return carry

    lax.fori_loop(0, DOFS // ROWS, rows, 0)


def start_kernel(state_ref, owner_ref, pick_ref, flags_ref, u_ref, payload_ref, slot_ref, *send_refs):
    u = state_ref[...].T
    u_ref[...] = u
    write_faces(u.astype(BF16), pick_ref, flags_ref, payload_ref, send_refs)
    before = lax.broadcasted_iota(jnp.int32, (TILE, TILE), 0) < lax.broadcasted_iota(jnp.int32, (TILE, TILE), 1)
    before = jnp.where(before, 1.0, 0.0).astype(BF16)
    owners = lax.broadcasted_iota(jnp.int32, (128, TILE), 0)
    carry = jnp.zeros((128, 1), F32)
    for t in range(TILES):
        owner = owner_ref[:, TILE * t : TILE * (t + 1)]
        match = jnp.where(owners == owner, 1.0, 0.0)
        earlier = dot(match.astype(BF16), before) + carry
        rank = jnp.sum(earlier * match, axis=0, keepdims=True)
        slot_ref[:, TILE * t : TILE * (t + 1)] = owner * CAP + rank.astype(jnp.int32)
        carry = carry + jnp.sum(match, axis=1, keepdims=True)


def push_kernel(matrix_ref, u_ref, pushed_ref):
    work = u_ref[...].astype(BF16).astype(F32)
    apply_matrices(matrix_ref, work, pushed_ref)


def update(step, matrix_ref, u_ref, pushed_ref, low_ref, high_ref, payload_ref, halo_refs, spread_ref, incoming_ref, flux_ref, change_ref):
    @pl.when(step == 0)
    def _():
        incoming_flux(payload_ref, halo_refs, spread_ref, incoming_ref, flux_ref)

    lanes = pl.ds(pl.multiple_of(step * TILE, TILE), TILE)
    rhs = (pushed_ref[...] + flux_ref[:, lanes]).astype(BF16).astype(F32)
    apply_matrices(matrix_ref, rhs, change_ref)
    moved = u_ref[...] + change_ref[...]
    return lanes, jnp.minimum(jnp.maximum(moved, low_ref[...].T), high_ref[...].T)


def step_kernel(matrix_ref, u_ref, pushed_ref, low_ref, high_ref, payload_ref, *rest):
    halo_refs, (spread_ref, pick_ref, flags_ref), rest = rest[:6], rest[6:9], rest[9:]
    (next_ref, next_payload_ref), send_refs, rest = rest[:2], rest[2:8], rest[8:]
    incoming_ref, flux_ref, change_ref, work_ref = rest
    step = pl.program_id(0)
    lanes, u = update(
        step, matrix_ref, u_ref, pushed_ref, low_ref, high_ref, payload_ref, halo_refs, spread_ref, incoming_ref, flux_ref, change_ref
    )
    next_ref[...] = u
    work_ref[:, lanes] = u.astype(BF16)

    @pl.when(step == TILES - 1)
    def _():
        write_faces(work_ref[...], pick_ref, flags_ref, next_payload_ref, send_refs)


def last_kernel(matrix_ref, u_ref, pushed_ref, low_ref, high_ref, payload_ref, *rest):
    halo_refs, (spread_ref, slot_ref), rest = rest[:6], rest[6:8], rest[8:]
    outgoing_ref, incoming_ref, flux_ref, change_ref, work_ref = rest
    step = pl.program_id(0)
    lanes, u = update(
        step, matrix_ref, u_ref, pushed_ref, low_ref, high_ref, payload_ref, halo_refs, spread_ref, incoming_ref, flux_ref, change_ref
    )
    work_ref[:, lanes] = u.astype(BF16)

    @pl.when(step == TILES - 1)
    def _():
        chunk = 256
        slot = slot_ref[...]
        work = work_ref[...]

        def place(n, carry):
            first = pl.multiple_of(n * chunk, chunk)
            rows = lax.broadcasted_iota(jnp.int32, (chunk, ZONES), 0) + first
            match = jnp.where(rows == slot, 1.0, 0.0).astype(BF16)
            taken = lax.dot_general(match, work, (((1,), (1,)), ((), ())), preferred_element_type=F32)
            outgoing_ref[pl.ds(first, chunk), :] = taken.astype(BF16)
            return carry

        lax.fori_loop(0, outgoing_ref.shape[0] // chunk, place, 0)


def whole(shape):
    return pl.BlockSpec(shape, lambda t: (0,) * len(shape))


MATRIX = pl.BlockSpec((TILE, DOFS * DOFS), lambda t: (t, 0))
ROWMAJOR = pl.BlockSpec((TILE, WIDTH), lambda t: (t, 0))
COLUMNS = pl.BlockSpec((WIDTH, TILE), lambda t: (0, t))
SMEM = pl.BlockSpec(memory_space=pltpu.SMEM)
SEQUENTIAL = pltpu.CompilerParams(dimension_semantics=("arbitrary",))
TRANSPOSED = jax.ShapeDtypeStruct((WIDTH, ZONES), F32)
PAYLOAD = jax.ShapeDtypeStruct((6 * FACE, ZONES), BF16)
SEND_SHAPES = [jax.ShapeDtypeStruct(s, BF16) for s in SENDS]
UPDATE_SCRATCH = [
    pltpu.VMEM((6 * FACE, ZONES), BF16),
    pltpu.VMEM((WIDTH, ZONES), F32),
    pltpu.VMEM((WIDTH, TILE), F32),
    pltpu.VMEM((WIDTH, ZONES), BF16),
]


def begin(state, owner, pick, flags):
    return pl.pallas_call(
        start_kernel,
        in_specs=[pl.BlockSpec(memory_space=pltpu.VMEM)] * 3 + [SMEM],
        out_shape=[TRANSPOSED, PAYLOAD, jax.ShapeDtypeStruct((1, ZONES), jnp.int32)] + SEND_SHAPES,
        name="begin",
    )(state, owner, pick, flags)


def push(convection, u):
    return pl.pallas_call(
        push_kernel,
        grid=(TILES,),
        in_specs=[MATRIX, COLUMNS],
        out_specs=COLUMNS,
        out_shape=TRANSPOSED,
        compiler_params=SEQUENTIAL,
        name="push",
    )(convection, u)


UPDATE_SPECS = [MATRIX, COLUMNS, COLUMNS, ROWMAJOR, ROWMAJOR, whole((6 * FACE, ZONES))] + [whole(s) for s in SENDS]


def step_on(args, spread, pick, flags):
    return pl.pallas_call(
        step_kernel,
        grid=(TILES,),
        in_specs=UPDATE_SPECS + [whole((WIDTH, 6 * FACE)), whole((6 * FACE, WIDTH)), SMEM],
        out_specs=[COLUMNS, whole((6 * FACE, ZONES))] + [whole(s) for s in SENDS],
        out_shape=[TRANSPOSED, PAYLOAD] + SEND_SHAPES,
        scratch_shapes=UPDATE_SCRATCH,
        compiler_params=SEQUENTIAL,
        name="step_on",
    )(*args, spread, pick, flags)


def finish(args, spread, slot, slots):
    return pl.pallas_call(
        last_kernel,
        grid=(TILES,),
        in_specs=UPDATE_SPECS + [whole((WIDTH, 6 * FACE)), whole((1, ZONES))],
        out_specs=whole((slots, WIDTH)),
        out_shape=jax.ShapeDtypeStruct((slots, WIDTH), BF16),
        scratch_shapes=UPDATE_SCRATCH,
        compiler_params=SEQUENTIAL,
        name="finish",
    )(*args, spread, slot)


def exchange(sends):
    halos = []
    for k, send in enumerate(sends):
        axis = AXES[k // 2]
        count = lax.axis_size(axis)
        move = 1 if k % 2 == 0 else -1
        halos.append(lax.ppermute(send, axis, [(i, (i + move) % count) for i in range(count)]))
    return halos


def shards(state, convection, inverse_mass, face_coupling, lower_bound, upper_bound, new_owner):
    state = state.reshape(ZONES, WIDTH)
    convection = convection.reshape(ZONES, DOFS * DOFS)
    inverse_mass = inverse_mass.reshape(ZONES, DOFS * DOFS)
    lower_bound = lower_bound.reshape(ZONES, WIDTH)
    upper_bound = upper_bound.reshape(ZONES, WIDTH)
    owner = new_owner.reshape(1, ZONES)
    devices = lax.axis_size(AXES)
    identity = jnp.eye(COMP, dtype=BF16)
    blocks = face_coupling.reshape(6, 16, DOFS)
    spread = (blocks.transpose(2, 0, 1)[None, :, :, None, :] * identity[:, None, None, :, None]).reshape(WIDTH, 6 * FACE)
    pick = jnp.asarray(pick_table(), BF16)
    flags = []
    for axis in AXES:
        index = lax.axis_index(axis)
        flags += [index < lax.axis_size(axis) - 1, index > 0]
    flags = jnp.stack(flags).astype(jnp.int32)

    u, payload, slot, *sends = begin(state, owner, pick, flags)
    halos = exchange(sends)
    pushed = push(convection, u)
    args = (inverse_mass, u, pushed, lower_bound, upper_bound, payload, *halos)
    u, payload, *sends = step_on(args, spread, pick, flags)
    halos = exchange(sends)
    pushed = push(convection, u)
    args = (inverse_mass, u, pushed, lower_bound, upper_bound, payload, *halos)
    outgoing = finish(args, spread, slot, devices * CAP)
    arrived = lax.all_to_all(outgoing.reshape(devices, CAP, WIDTH), AXES, split_axis=0, concat_axis=0, tiled=True)
    return arrived.reshape(devices * CAP, WIDTH).astype(F32)


def solution(mesh):
    in_specs = (
        P("gx", "gy", "gz", None),
        P("gx", "gy", "gz", None),
        P("gx", "gy", "gz", None),
        P(),
        P("gx", "gy", "gz", None),
        P("gx", "gy", "gz", None),
        P(AXES, None, None),
    )
    out_specs = P(AXES, None)
    return jax.shard_map(shards, mesh=mesh, in_specs=in_specs, out_specs=out_specs, check_vma=False)
```

```python
import jax
import jax.numpy as jnp
import numpy as np
from jax import lax
from jax.experimental import pallas as pl
from jax.experimental.pallas import tpu as pltpu
from jax.sharding import PartitionSpec as P

COMP = 4
DOFS = 64
STEPS = 2
WIDTH = COMP * DOFS
EX, EY, EZ = 4, 8, 32
ZONES = EX * EY * EZ
PLANE = EY * EZ
TILE = 128
TILES = ZONES // TILE
GROUP = 16
FACE = COMP * 16
CAP = 16
AXES = ("gx", "gy", "gz")
F32 = jnp.float32
BF16 = jnp.bfloat16
ORDER = np.arange(WIDTH).reshape(COMP, DOFS // 2, 2).transpose(1, 0, 2).reshape(WIDTH)


def pick_table():
    table = np.zeros((6, COMP, 16, COMP, 4, 4, 4), np.float32)
    for c in range(COMP):
        for f in range(16):
            p, q = f // 4, f % 4
            for side, level in ((0, 3), (1, 0)):
                table[0 + side, c, f, c, level, p, q] = 1
                table[2 + side, c, f, c, p, level, q] = 1
                table[4 + side, c, f, c, p, q, level] = 1
    return table.reshape(6 * FACE, WIDTH)[:, ORDER]


def expand_table():
    table = np.zeros((COMP, DOFS, WIDTH * 2), np.float32)
    for n, c in enumerate((0, 1, 2, 3, 1, 0, 3, 2)):
        table[c, :, DOFS * n : DOFS * (n + 1)] = np.eye(DOFS)
    return table.reshape(WIDTH, 2 * WIDTH)[ORDER]


def coupling_tables():
    rows = np.tile(np.eye(DOFS, dtype=np.float32), (COMP, 1))[ORDER]
    columns = np.zeros((6, 16, 6, COMP, 16), np.float32)
    for k in range(6):
        for f in range(16):
            columns[k, f, k, :, f] = 1
    return rows, columns.reshape(96, 6 * FACE)


def order_table():
    return np.eye(WIDTH, dtype=np.float32)[:, ORDER]


def dot(a, b):
    return jnp.dot(a, b, preferred_element_type=F32)


def select_zones(zone_of, count):
    column = lax.broadcasted_iota(jnp.int32, (1, 128), 1)
    wanted = jnp.where(column < count, zone_of(column), -1)
    zone = lax.broadcasted_iota(jnp.int32, (ZONES, 128), 0)
    return jnp.where(zone == wanted, 1.0, 0.0).astype(BF16)


def place_zones(zone_of, count):
    row = lax.broadcasted_iota(jnp.int32, (128, 1), 0)
    wanted = jnp.where(row < count, zone_of(row), -1)
    zone = lax.broadcasted_iota(jnp.int32, (128, ZONES), 1)
    return jnp.where(zone == wanted, 1.0, 0.0).astype(BF16)


def y_zone(level):
    return lambda n: (n // EZ) * PLANE + level * EZ + n % EZ


def z_zone(level):
    return lambda n: n * EZ + level


SENDS = ((64, 256), (64, 256), (64, 128), (64, 128), (64, 128), (64, 128))


def write_faces(work, pick, payload_ref, send_refs):
    payload = dot(pick, work).astype(BF16)
    payload_ref[...] = payload

    def face(k):
        return payload[FACE * k : FACE * (k + 1)]

    pieces = (
        face(0)[:, ZONES - PLANE :].astype(F32),
        face(1)[:, :PLANE].astype(F32),
        dot(face(2), select_zones(y_zone(EY - 1), EX * EZ)),
        dot(face(3), select_zones(y_zone(0), EX * EZ)),
        dot(face(4), select_zones(z_zone(EZ - 1), EX * EY)),
        dot(face(5), select_zones(z_zone(0), EX * EY)),
    )
    for k in range(6):
        index = lax.axis_index(AXES[k // 2])
        inner = index > 0 if k % 2 else index < lax.axis_size(AXES[k // 2]) - 1
        send_refs[k][...] = jnp.where(inner, pieces[k], 0.0).astype(BF16)


def incoming_flux(payload_ref, halo_refs, spread_ref, incoming_ref):
    def face(k):
        return payload_ref[FACE * k : FACE * (k + 1), :]

    incoming_ref[0:FACE, 0:PLANE] = halo_refs[0][...]
    incoming_ref[0:FACE, PLANE:ZONES] = payload_ref[0:FACE, 0 : ZONES - PLANE]
    incoming_ref[FACE : 2 * FACE, 0 : ZONES - PLANE] = payload_ref[FACE : 2 * FACE, PLANE:ZONES]
    incoming_ref[FACE : 2 * FACE, ZONES - PLANE : ZONES] = halo_refs[1][...]
    zone = lax.broadcasted_iota(jnp.int32, (FACE, ZONES), 1)
    third = zone % EZ
    second = zone // EZ % EY
    cases = (
        (2, EZ, second == 0, y_zone(0), EX * EZ),
        (3, ZONES - EZ, second == EY - 1, y_zone(EY - 1), EX * EZ),
        (4, 1, third == 0, z_zone(0), EX * EY),
        (5, ZONES - 1, third == EZ - 1, z_zone(EZ - 1), EX * EY),
    )
    for k, shift, edge, zone_of, count in cases:
        moved = pltpu.roll(face(k).astype(F32), shift, 1)
        placed = dot(halo_refs[k][...], place_zones(zone_of, count))
        incoming_ref[FACE * k : FACE * (k + 1), :] = jnp.where(edge, placed, moved).astype(BF16)
    return dot(spread_ref[...], incoming_ref[...])


def swap_blocks(parts, axis, block):
    size = parts[0].shape[axis]
    place = lax.broadcasted_iota(jnp.int32, parts[0].shape, axis) // block
    parts = list(parts)
    half = len(parts) // 2
    while half:
        low = (place & half) == 0
        for v in range(len(parts)):
            if v & half == 0:
                a, b = parts[v], parts[v + half]
                parts[v] = jnp.where(low, a, pltpu.roll(b, half * block, axis))
                parts[v + half] = jnp.where(low, pltpu.roll(a, size - half * block, axis), b)
        half //= 2
    return parts


def turned(rows):
    columns = rows.T
    parts = []
    for k in range(DOFS // 8):
        parts += swap_blocks([columns[DOFS * c + 8 * k : DOFS * c + 8 * k + 8] for c in range(COMP)], 0, 2)
    return parts


def tile(t):
    return pl.ds(pl.multiple_of(t * TILE, TILE), TILE)


def fetches(pairs, sems, first=0):
    return [pltpu.make_async_copy(source, target, sems.at[first + n]) for n, (source, target) in enumerate(pairs)]


def fetch_tile(source_ref, target_ref, sems, t):
    return pltpu.make_async_copy(source_ref.at[tile(t)], target_ref.at[tile(t)], sems.at[t])


def apply_matrices(wait, matrix_ref, values_ref, expand_ref, left_ref, product_ref, emit):
    def expand(t, carry):
        expanded = lax.dot_general(
            values_ref[:, pl.ds(pl.multiple_of(t * 2 * TILE, 2 * TILE), 2 * TILE)],
            expand_ref[...],
            (((0,), (0,)), ((), ())),
            preferred_element_type=F32,
        )
        for n in range(8):
            c, s = n // 2, n % 2
            source = c // 2 + (0 if c % 2 == s else 2)
            left_ref[pl.ds(t * 16 * TILE + n, 2 * TILE, stride=8), :] = expanded[:, TILE * source : TILE * (source + 1)]
        return carry

    lax.fori_loop(0, TILES // 2, expand, 0)
    zone = lax.broadcasted_iota(jnp.int32, (8, DOFS // 2 * GROUP), 1) % GROUP
    shape = (8 * GROUP, TILE)
    half = lax.broadcasted_iota(jnp.int32, shape, 0) % 2 == lax.broadcasted_iota(jnp.int32, shape, 1) // DOFS

    def apply(t, carry):
        wait(t)
        for g in range(TILE // GROUP):
            first = pl.multiple_of(t * TILE + GROUP * g, GROUP)
            left = jnp.where(half, left_ref[pl.ds(pl.multiple_of(8 * first, 8 * GROUP), 8 * GROUP), :], 0.0).astype(BF16)
            matrix = matrix_ref[pl.ds(first, GROUP), :]
            right = jnp.concatenate([matrix[:, TILE * m : TILE * (m + 1)] for m in range(DOFS // 2)], axis=0)
            product = lax.dot_general(left, right, (((1,), (1,)), ((), ())), preferred_element_type=F32)
            kept = product[0:8]
            for z in range(1, GROUP):
                kept = jnp.where(zone == z, product[8 * z : 8 * z + 8], kept)
            product_ref[8 * g : 8 * g + 8, :] = kept
        for q in range(4):
            parts = [product_ref[8 * g : 8 * g + 8, TILE * q : TILE * (q + 1)] for g in range(TILE // GROUP)]
            for n, part in enumerate(swap_blocks(parts, 1, GROUP)):
                emit(t, 8 * q + n, part)
        return carry

    lax.fori_loop(0, TILES, apply, 0)


def start_kernel(*refs):
    sources, (u_ref, work_ref, payload_ref, slot_ref, spread_ref), send_refs = refs[:6], refs[6:11], refs[11:17]
    targets, sems = refs[17:23], refs[23]
    state_ref, pick_ref, owner_ref, coupling_ref, rows_ref, columns_ref = targets
    copies = fetches(list(zip(sources, targets)), sems)
    for copy in copies:
        copy.start()
    copies[0].wait()
    for t in range(TILES):
        lanes = slice(TILE * t, TILE * (t + 1))
        for m, part in enumerate(turned(state_ref[lanes, :])):
            u_ref[8 * m : 8 * m + 8, lanes] = part
    work = u_ref[...].astype(BF16)
    work_ref[...] = work
    copies[1].wait()
    write_faces(work, pick_ref[...], payload_ref, send_refs)
    for copy in copies[2:]:
        copy.wait()
    before = lax.broadcasted_iota(jnp.int32, (TILE, TILE), 0) < lax.broadcasted_iota(jnp.int32, (TILE, TILE), 1)
    before = jnp.where(before, 1.0, 0.0).astype(BF16)
    owners = lax.broadcasted_iota(jnp.int32, (128, TILE), 0)
    carry = jnp.zeros((128, 1), F32)
    for t in range(TILES):
        owner = owner_ref[:, TILE * t : TILE * (t + 1)]
        match = jnp.where(owners == owner, 1.0, 0.0)
        earlier = dot(match.astype(BF16), before) + carry
        rank = jnp.sum(earlier * match, axis=0, keepdims=True)
        slot_ref[:, TILE * t : TILE * (t + 1)] = owner * CAP + rank.astype(jnp.int32)
        carry = carry + jnp.sum(match, axis=1, keepdims=True)
    entries = dot(rows_ref[...], coupling_ref[...])
    entries = dot(entries.astype(BF16), columns_ref[...])
    own = lax.broadcasted_iota(jnp.int32, entries.shape, 0) // 2 % COMP
    theirs = lax.broadcasted_iota(jnp.int32, entries.shape, 1) // 16 % COMP
    spread_ref[...] = jnp.where(own == theirs, entries, 0.0).astype(BF16)


def push_kernel(matrix_source, expand_source, work_ref, pushed_ref, *scratch):
    left_ref, product_ref, matrix_ref, expand_ref, sems = scratch
    (expanded,) = fetches([(expand_source, expand_ref)], sems, TILES)
    expanded.start()
    for t in range(TILES):
        fetch_tile(matrix_source, matrix_ref, sems, t).start()
    expanded.wait()

    def emit(t, m, part):
        pushed_ref[8 * m : 8 * m + 8, tile(t)] = part

    def wait(t):
        fetch_tile(matrix_source, matrix_ref, sems, t).wait()

    apply_matrices(wait, matrix_ref, work_ref, expand_ref, left_ref, product_ref, emit)


def update(sources, fields, halo_refs, next_ref, scratch):
    u_ref, pushed_ref, payload_ref, spread_ref = fields
    incoming_ref, rhs_ref, left_ref, product_ref, matrix_ref, expand_ref, sems = scratch[:7]
    lower_ref, upper_ref, low_ref, high_ref, table_ref = scratch[7:]
    expanded, low, high, table = fetches(
        [(sources[3], expand_ref), (sources[1], low_ref), (sources[2], high_ref), (sources[4], table_ref)], sems, TILES
    )
    for copy in (expanded, low, high):
        copy.start()
    for t in range(TILES):
        fetch_tile(sources[0], matrix_ref, sems, t).start()
    table.start()
    rhs_ref[...] = (pushed_ref[...] + incoming_flux(payload_ref, halo_refs, spread_ref, incoming_ref)).astype(BF16)
    low.wait()
    high.wait()

    def bounds(t, carry):
        for m, part in enumerate(turned(low_ref[tile(t), :])):
            lower_ref[8 * m : 8 * m + 8, tile(t)] = part
        for m, part in enumerate(turned(high_ref[tile(t), :])):
            upper_ref[8 * m : 8 * m + 8, tile(t)] = part
        return carry

    lax.fori_loop(0, TILES, bounds, 0)
    expanded.wait()

    def emit(t, m, part):
        rows = slice(8 * m, 8 * m + 8)
        moved = u_ref[rows, tile(t)] + part
        next_ref[rows, tile(t)] = jnp.minimum(jnp.maximum(moved, lower_ref[rows, tile(t)]), upper_ref[rows, tile(t)])

    def wait(t):
        fetch_tile(sources[0], matrix_ref, sems, t).wait()

    apply_matrices(wait, matrix_ref, rhs_ref, expand_ref, left_ref, product_ref, emit)
    table.wait()
    return table_ref[...]


def step_kernel(*refs):
    sources, fields, halo_refs, refs = refs[:5], refs[5:9], refs[9:15], refs[15:]
    (next_ref, work_ref, next_payload_ref), send_refs, scratch = refs[:3], refs[3:9], refs[9:]
    pick = update(sources, fields, halo_refs, next_ref, scratch)
    work = next_ref[...].astype(BF16)
    work_ref[...] = work
    write_faces(work, pick, next_payload_ref, send_refs)


def last_kernel(*refs):
    sources, fields, halo_refs, slot_ref, refs = refs[:5], refs[5:9], refs[9:15], refs[15], refs[16:]
    outgoing_ref, next_ref, scratch = refs[0], refs[1], refs[2:]
    order = update(sources, fields, halo_refs, next_ref, scratch)
    chunk = 256
    slot = slot_ref[...]
    work = dot(order, next_ref[...].astype(BF16)).astype(BF16)

    def place(n, carry):
        first = pl.multiple_of(n * chunk, chunk)
        rows = lax.broadcasted_iota(jnp.int32, (chunk, ZONES), 0) + first
        match = jnp.where(rows == slot, 1.0, 0.0).astype(BF16)
        taken = lax.dot_general(match, work, (((1,), (1,)), ((), ())), preferred_element_type=F32)
        outgoing_ref[pl.ds(first, chunk), :] = taken.astype(BF16)
        return carry

    lax.fori_loop(0, outgoing_ref.shape[0] // chunk, place, 0)


INNER = pl.BlockSpec(memory_space=pltpu.VMEM)
SEND_SHAPES = [jax.ShapeDtypeStruct(s, BF16) for s in SENDS]
STATE = pltpu.VMEM((WIDTH, ZONES), F32)
WORK = pltpu.VMEM((WIDTH, ZONES), BF16)
PAYLOAD = pltpu.VMEM((6 * FACE, ZONES), BF16)
APPLY_SCRATCH = [
    pltpu.VMEM((8 * ZONES, TILE), F32),
    pltpu.VMEM((TILE // GROUP * 8, DOFS // 2 * GROUP), F32),
    pltpu.VMEM((ZONES, DOFS * DOFS), BF16),
    pltpu.VMEM((WIDTH, 2 * WIDTH), BF16),
    pltpu.SemaphoreType.DMA((TILES + 4,)),
]
ROWMAJOR = pltpu.VMEM((ZONES, WIDTH), F32)
UPDATE_SCRATCH = [PAYLOAD, WORK, *APPLY_SCRATCH, STATE, STATE, ROWMAJOR, ROWMAJOR]


def call(kernel, name, sources, args, out_shape, scratch_shapes, limit):
    args = [pltpu.with_memory_space_constraint(a, pltpu.VMEM) for a in args]
    sources = [pltpu.with_memory_space_constraint(a, pltpu.HBM) for a in sources]
    return pl.pallas_call(
        kernel,
        in_specs=[pl.BlockSpec(memory_space=pltpu.HBM)] * len(sources) + [INNER] * len(args),
        out_shape=out_shape,
        scratch_shapes=scratch_shapes,
        compiler_params=pltpu.CompilerParams(vmem_limit_bytes=limit << 20),
        name=name,
    )(*sources, *args)


def exchange(sends):
    halos = []
    for k, send in enumerate(sends):
        axis = AXES[k // 2]
        count = lax.axis_size(axis)
        move = 1 if k % 2 == 0 else -1
        halos.append(lax.ppermute(send, axis, [(i, (i + move) % count) for i in range(count)]))
    return halos


def shards(state, convection, inverse_mass, face_coupling, lower_bound, upper_bound, new_owner):
    state = state.reshape(ZONES, WIDTH)
    convection = convection.reshape(ZONES, DOFS * DOFS)
    inverse_mass = inverse_mass.reshape(ZONES, DOFS * DOFS)
    lower_bound = lower_bound.reshape(ZONES, WIDTH)
    upper_bound = upper_bound.reshape(ZONES, WIDTH)
    owner = new_owner.reshape(1, ZONES)
    devices = lax.axis_size(AXES)
    pick, expand, order, rows, columns = [
        jnp.asarray(t, BF16) for t in (pick_table(), expand_table(), order_table(), *coupling_tables())
    ]
    slots = pltpu.VMEM((1, ZONES), jnp.int32)
    table = pltpu.VMEM((WIDTH, 6 * FACE), BF16)
    sources = (state, pick, owner, face_coupling.T, rows, columns)
    state, work, payload, slot, spread, *sends = call(
        start_kernel,
        "begin",
        sources,
        (),
        [STATE, WORK, PAYLOAD, slots, table] + SEND_SHAPES,
        [pltpu.VMEM(a.shape, a.dtype) for a in sources] + [pltpu.SemaphoreType.DMA((len(sources),))],
        8,
    )
    for step in range(STEPS):
        halos = exchange(sends)
        pushed = call(push_kernel, "push", (convection, expand), (work,), STATE, APPLY_SCRATCH, 16)
        sources = (inverse_mass, lower_bound, upper_bound, expand)
        fields = (state, pushed, payload, spread, *halos)
        if step < STEPS - 1:
            state, work, payload, *sends = call(
                step_kernel,
                "step_on",
                (*sources, pick),
                fields,
                [STATE, WORK, PAYLOAD] + SEND_SHAPES,
                [*UPDATE_SCRATCH, pltpu.VMEM(pick.shape, BF16)],
                24,
            )
    outgoing = call(
        last_kernel,
        "finish",
        (*sources, order),
        (*fields, slot),
        jax.ShapeDtypeStruct((devices * CAP, WIDTH), BF16),
        [STATE, *UPDATE_SCRATCH, pltpu.VMEM(order.shape, BF16)],
        24,
    )
    arrived = lax.all_to_all(outgoing.reshape(devices, CAP, WIDTH), AXES, split_axis=0, concat_axis=0, tiled=True)
    return arrived.reshape(devices * CAP, WIDTH).astype(F32)


def solution(mesh):
    in_specs = (
        P("gx", "gy", "gz", None),
        P("gx", "gy", "gz", None),
        P("gx", "gy", "gz", None),
        P(),
        P("gx", "gy", "gz", None),
        P("gx", "gy", "gz", None),
        P(AXES, None, None),
    )
    out_specs = P(AXES, None)
    return jax.shard_map(shards, mesh=mesh, in_specs=in_specs, out_specs=out_specs, check_vma=False)
```

```python
import jax
import jax.numpy as jnp
import numpy as np
from jax import lax
from jax.experimental import pallas as pl
from jax.experimental.pallas import tpu as pltpu
from jax.sharding import PartitionSpec as P

COMP = 4
DOFS = 64
STEPS = 2
WIDTH = COMP * DOFS
EX, EY, EZ = 4, 8, 32
ZONES = EX * EY * EZ
PLANE = EY * EZ
TILE = 128
TILES = ZONES // TILE
GROUP = 16
FACE = COMP * 16
CAP = 16
AXES = ("gx", "gy", "gz")
F32 = jnp.float32
BF16 = jnp.bfloat16
ORDER = np.arange(WIDTH).reshape(COMP, DOFS // 2, 2).transpose(1, 0, 2).reshape(WIDTH)


def pick_table():
    table = np.zeros((6, COMP, 16, COMP, 4, 4, 4), np.float32)
    for c in range(COMP):
        for f in range(16):
            p, q = f // 4, f % 4
            for side, level in ((0, 3), (1, 0)):
                table[0 + side, c, f, c, level, p, q] = 1
                table[2 + side, c, f, c, p, level, q] = 1
                table[4 + side, c, f, c, p, q, level] = 1
    return table.reshape(6 * FACE, WIDTH)[:, ORDER]


def expand_table():
    table = np.zeros((COMP, DOFS, WIDTH * 2), np.float32)
    for n, c in enumerate((0, 1, 2, 3, 1, 0, 3, 2)):
        table[c, :, DOFS * n : DOFS * (n + 1)] = np.eye(DOFS)
    return table.reshape(WIDTH, 2 * WIDTH)[ORDER]


def coupling_tables():
    rows = np.tile(np.eye(DOFS, dtype=np.float32), (COMP, 1))[ORDER]
    columns = np.zeros((6, 16, 6, COMP, 16), np.float32)
    for k in range(6):
        for f in range(16):
            columns[k, f, k, :, f] = 1
    return rows, columns.reshape(96, 6 * FACE)


def order_table():
    return np.eye(WIDTH, dtype=np.float32)[:, ORDER]


def dot(a, b):
    return jnp.dot(a, b, preferred_element_type=F32)


def select_zones(zone_of, count):
    column = lax.broadcasted_iota(jnp.int32, (1, 128), 1)
    wanted = jnp.where(column < count, zone_of(column), -1)
    zone = lax.broadcasted_iota(jnp.int32, (ZONES, 128), 0)
    return jnp.where(zone == wanted, 1.0, 0.0).astype(BF16)


def place_zones(zone_of, count):
    row = lax.broadcasted_iota(jnp.int32, (128, 1), 0)
    wanted = jnp.where(row < count, zone_of(row), -1)
    zone = lax.broadcasted_iota(jnp.int32, (128, ZONES), 1)
    return jnp.where(zone == wanted, 1.0, 0.0).astype(BF16)


def y_zone(level):
    return lambda n: (n // EZ) * PLANE + level * EZ + n % EZ


def z_zone(level):
    return lambda n: n * EZ + level


SENDS = ((64, 256), (64, 256), (64, 128), (64, 128), (64, 128), (64, 128))


def write_faces(work, pick, payload_ref, send_refs):
    payload = dot(pick, work).astype(BF16)
    payload_ref[...] = payload

    def face(k):
        return payload[FACE * k : FACE * (k + 1)]

    pieces = (
        face(0)[:, ZONES - PLANE :].astype(F32),
        face(1)[:, :PLANE].astype(F32),
        dot(face(2), select_zones(y_zone(EY - 1), EX * EZ)),
        dot(face(3), select_zones(y_zone(0), EX * EZ)),
        dot(face(4), select_zones(z_zone(EZ - 1), EX * EY)),
        dot(face(5), select_zones(z_zone(0), EX * EY)),
    )
    for k in range(6):
        index = lax.axis_index(AXES[k // 2])
        inner = index > 0 if k % 2 else index < lax.axis_size(AXES[k // 2]) - 1
        send_refs[k][...] = jnp.where(inner, pieces[k], 0.0).astype(BF16)


def incoming_flux(payload_ref, halo_refs, spread_ref, incoming_ref):
    def face(k):
        return payload_ref[FACE * k : FACE * (k + 1), :]

    incoming_ref[0:FACE, 0:PLANE] = halo_refs[0][...]
    incoming_ref[0:FACE, PLANE:ZONES] = payload_ref[0:FACE, 0 : ZONES - PLANE]
    incoming_ref[FACE : 2 * FACE, 0 : ZONES - PLANE] = payload_ref[FACE : 2 * FACE, PLANE:ZONES]
    incoming_ref[FACE : 2 * FACE, ZONES - PLANE : ZONES] = halo_refs[1][...]
    zone = lax.broadcasted_iota(jnp.int32, (FACE, ZONES), 1)
    third = zone % EZ
    second = zone // EZ % EY
    cases = (
        (2, EZ, second == 0, y_zone(0), EX * EZ),
        (3, ZONES - EZ, second == EY - 1, y_zone(EY - 1), EX * EZ),
        (4, 1, third == 0, z_zone(0), EX * EY),
        (5, ZONES - 1, third == EZ - 1, z_zone(EZ - 1), EX * EY),
    )
    for k, shift, edge, zone_of, count in cases:
        moved = pltpu.roll(face(k).astype(F32), shift, 1)
        placed = dot(halo_refs[k][...], place_zones(zone_of, count))
        incoming_ref[FACE * k : FACE * (k + 1), :] = jnp.where(edge, placed, moved).astype(BF16)
    return dot(spread_ref[...], incoming_ref[...])


def swap_blocks(parts, axis, block):
    size = parts[0].shape[axis]
    place = lax.broadcasted_iota(jnp.int32, parts[0].shape, axis) // block
    parts = list(parts)
    half = len(parts) // 2
    while half:
        low = (place & half) == 0
        for v in range(len(parts)):
            if v & half == 0:
                a, b = parts[v], parts[v + half]
                parts[v] = jnp.where(low, a, pltpu.roll(b, half * block, axis))
                parts[v + half] = jnp.where(low, pltpu.roll(a, size - half * block, axis), b)
        half //= 2
    return parts


def turned(rows):
    columns = rows.T
    parts = []
    for k in range(DOFS // 8):
        parts += swap_blocks([columns[DOFS * c + 8 * k : DOFS * c + 8 * k + 8] for c in range(COMP)], 0, 2)
    return parts


def tile(t):
    return pl.ds(pl.multiple_of(t * TILE, TILE), TILE)


def fetches(pairs, sems, first=0):
    return [pltpu.make_async_copy(source, target, sems.at[first + n]) for n, (source, target) in enumerate(pairs)]


def fetch_tile(source_ref, target_ref, sems, t):
    return pltpu.make_async_copy(source_ref.at[tile(t)], target_ref.at[tile(t)], sems.at[t])


def apply_matrices(wait, prepare, matrix_ref, values_ref, expand_ref, left_refs, product_refs, emit):
    zone = lax.broadcasted_iota(jnp.int32, (8, DOFS // 2 * GROUP), 1) % GROUP
    shape = (8 * GROUP, TILE)
    half = lax.broadcasted_iota(jnp.int32, shape, 0) % 2 == lax.broadcasted_iota(jnp.int32, shape, 1) // DOFS

    def expand(t, left_ref):
        expanded = lax.dot_general(
            values_ref[:, tile(t)], expand_ref[...], (((0,), (0,)), ((), ())), preferred_element_type=F32
        )
        for n in range(8):
            c, s = n // 2, n % 2
            source = c // 2 + (0 if c % 2 == s else 2)
            left_ref[pl.ds(n, TILE, stride=8), :] = expanded[:, TILE * source : TILE * (source + 1)]

    def multiply(t, left_ref, product_ref):
        for g in range(TILE // GROUP):
            left = jnp.where(half, left_ref[8 * GROUP * g : 8 * GROUP * (g + 1), :], 0.0).astype(BF16)
            matrix = matrix_ref[pl.ds(pl.multiple_of(t * TILE + GROUP * g, GROUP), GROUP), :]
            right = jnp.concatenate([matrix[:, TILE * m : TILE * (m + 1)] for m in range(DOFS // 2)], axis=0)
            product = lax.dot_general(left, right, (((1,), (1,)), ((), ())), preferred_element_type=F32)
            kept = product[0:8]
            for z in range(1, GROUP):
                kept = jnp.where(zone == z, product[8 * z : 8 * z + 8], kept)
            product_ref[8 * g : 8 * g + 8, :] = kept

    def settle(t, slot):
        product_ref = product_refs[slot]
        for q in range(4):
            parts = [product_ref[8 * g : 8 * g + 8, TILE * q : TILE * (q + 1)] for g in range(TILE // GROUP)]
            for n, part in enumerate(swap_blocks(parts, 1, GROUP)):
                emit(t, slot, 8 * q + n, part)

    (even_left, odd_left), (even_product, odd_product) = left_refs, product_refs
    expand(0, even_left)
    odd_product[...] = jnp.zeros_like(odd_product)

    def pair(n, carry):
        t = 2 * n
        wait(t)
        wait(t + 1)
        settle(jnp.maximum(t - 1, 0), 1)
        prepare(t, 0)
        expand(t + 1, odd_left)
        multiply(t, even_left, even_product)
        settle(t, 0)
        prepare(t + 1, 1)
        expand(jnp.minimum(t + 2, TILES - 1), even_left)
        multiply(t + 1, odd_left, odd_product)
        return carry

    lax.fori_loop(0, TILES // 2, pair, 0)
    settle(TILES - 1, 1)


def start_kernel(*refs):
    sources, (u_ref, work_ref, payload_ref, slot_ref, spread_ref), send_refs = refs[:6], refs[6:11], refs[11:17]
    targets, sems = refs[17:23], refs[23]
    state_ref, pick_ref, owner_ref, coupling_ref, rows_ref, columns_ref = targets
    copies = fetches(list(zip(sources, targets)), sems)
    for copy in copies:
        copy.start()
    copies[0].wait()
    for t in range(TILES):
        lanes = slice(TILE * t, TILE * (t + 1))
        for m, part in enumerate(turned(state_ref[lanes, :])):
            u_ref[8 * m : 8 * m + 8, lanes] = part
    work = u_ref[...].astype(BF16)
    work_ref[...] = work
    copies[1].wait()
    write_faces(work, pick_ref[...], payload_ref, send_refs)
    for copy in copies[2:]:
        copy.wait()
    before = lax.broadcasted_iota(jnp.int32, (TILE, TILE), 0) < lax.broadcasted_iota(jnp.int32, (TILE, TILE), 1)
    before = jnp.where(before, 1.0, 0.0).astype(BF16)
    owners = lax.broadcasted_iota(jnp.int32, (128, TILE), 0)
    carry = jnp.zeros((128, 1), F32)
    for t in range(TILES):
        owner = owner_ref[:, TILE * t : TILE * (t + 1)]
        match = jnp.where(owners == owner, 1.0, 0.0)
        earlier = dot(match.astype(BF16), before) + carry
        rank = jnp.sum(earlier * match, axis=0, keepdims=True)
        slot_ref[:, TILE * t : TILE * (t + 1)] = owner * CAP + rank.astype(jnp.int32)
        carry = carry + jnp.sum(match, axis=1, keepdims=True)
    entries = dot(rows_ref[...], coupling_ref[...])
    entries = dot(entries.astype(BF16), columns_ref[...])
    own = lax.broadcasted_iota(jnp.int32, entries.shape, 0) // 2 % COMP
    theirs = lax.broadcasted_iota(jnp.int32, entries.shape, 1) // 16 % COMP
    spread_ref[...] = jnp.where(own == theirs, entries, 0.0).astype(BF16)


def push_kernel(matrix_source, expand_source, work_ref, pushed_ref, *scratch):
    left_refs, product_refs, (matrix_ref, expand_ref, sems) = scratch[0:2], scratch[2:4], scratch[4:7]
    (expanded,) = fetches([(expand_source, expand_ref)], sems, TILES)
    expanded.start()
    for t in range(TILES):
        fetch_tile(matrix_source, matrix_ref, sems, t).start()
    expanded.wait()

    def emit(t, slot, m, part):
        pushed_ref[8 * m : 8 * m + 8, tile(t)] = part

    def wait(t):
        fetch_tile(matrix_source, matrix_ref, sems, t).wait()

    apply_matrices(wait, lambda t, slot: None, matrix_ref, work_ref, expand_ref, left_refs, product_refs, emit)


def update(sources, fields, halo_refs, next_ref, scratch):
    u_ref, pushed_ref, payload_ref, spread_ref = fields
    (incoming_ref, rhs_ref), left_refs, product_refs = scratch[0:2], scratch[2:4], scratch[4:6]
    (matrix_ref, expand_ref, sems), lower_refs, upper_refs = scratch[6:9], scratch[9:11], scratch[11:13]
    low_ref, high_ref, table_ref = scratch[13:]
    expanded, low, high, table = fetches(
        [(sources[3], expand_ref), (sources[1], low_ref), (sources[2], high_ref), (sources[4], table_ref)], sems, TILES
    )
    for copy in (expanded, low, high):
        copy.start()
    for t in range(TILES):
        fetch_tile(sources[0], matrix_ref, sems, t).start()
    table.start()
    rhs_ref[...] = (pushed_ref[...] + incoming_flux(payload_ref, halo_refs, spread_ref, incoming_ref)).astype(BF16)
    low.wait()
    high.wait()
    expanded.wait()

    def prepare(t, slot):
        for m, part in enumerate(turned(low_ref[tile(t), :])):
            lower_refs[slot][8 * m : 8 * m + 8, :] = part
        for m, part in enumerate(turned(high_ref[tile(t), :])):
            upper_refs[slot][8 * m : 8 * m + 8, :] = part

    def emit(t, slot, m, part):
        rows = slice(8 * m, 8 * m + 8)
        moved = u_ref[rows, tile(t)] + part
        next_ref[rows, tile(t)] = jnp.minimum(jnp.maximum(moved, lower_refs[slot][rows, :]), upper_refs[slot][rows, :])

    def wait(t):
        fetch_tile(sources[0], matrix_ref, sems, t).wait()

    apply_matrices(wait, prepare, matrix_ref, rhs_ref, expand_ref, left_refs, product_refs, emit)
    table.wait()
    return table_ref[...]


def step_kernel(*refs):
    sources, fields, halo_refs, refs = refs[:5], refs[5:9], refs[9:15], refs[15:]
    (next_ref, work_ref, next_payload_ref), send_refs, scratch = refs[:3], refs[3:9], refs[9:]
    pick = update(sources, fields, halo_refs, next_ref, scratch)
    work = next_ref[...].astype(BF16)
    work_ref[...] = work
    write_faces(work, pick, next_payload_ref, send_refs)


def last_kernel(*refs):
    sources, fields, halo_refs, slot_ref, refs = refs[:5], refs[5:9], refs[9:15], refs[15], refs[16:]
    outgoing_ref, next_ref, scratch = refs[0], refs[1], refs[2:]
    order = update(sources, fields, halo_refs, next_ref, scratch)
    chunk = 512
    slot = slot_ref[...]
    work = dot(order, next_ref[...].astype(BF16)).astype(BF16)

    def place(n, carry):
        first = pl.multiple_of(n * chunk, chunk)
        rows = lax.broadcasted_iota(jnp.int32, (chunk, ZONES), 0) + first
        match = jnp.where(rows == slot, 1.0, 0.0).astype(BF16)
        taken = lax.dot_general(match, work, (((1,), (1,)), ((), ())), preferred_element_type=F32)
        outgoing_ref[pl.ds(first, chunk), :] = taken.astype(BF16)
        return carry

    lax.fori_loop(0, outgoing_ref.shape[0] // chunk, place, 0)


INNER = pl.BlockSpec(memory_space=pltpu.VMEM)
SEND_SHAPES = [jax.ShapeDtypeStruct(s, BF16) for s in SENDS]
STATE = pltpu.VMEM((WIDTH, ZONES), F32)
WORK = pltpu.VMEM((WIDTH, ZONES), BF16)
PAYLOAD = pltpu.VMEM((6 * FACE, ZONES), BF16)
APPLY_SCRATCH = [
    *[pltpu.VMEM((8 * TILE, TILE), F32)] * 2,
    *[pltpu.VMEM((TILE // GROUP * 8, DOFS // 2 * GROUP), F32)] * 2,
    pltpu.VMEM((ZONES, DOFS * DOFS), BF16),
    pltpu.VMEM((WIDTH, 2 * WIDTH), BF16),
    pltpu.SemaphoreType.DMA((TILES + 4,)),
]
ROWMAJOR = pltpu.VMEM((ZONES, WIDTH), F32)
UPDATE_SCRATCH = [PAYLOAD, WORK, *APPLY_SCRATCH, *[pltpu.VMEM((WIDTH, TILE), F32)] * 4, ROWMAJOR, ROWMAJOR]


def call(kernel, name, sources, args, out_shape, scratch_shapes, limit):
    args = [pltpu.with_memory_space_constraint(a, pltpu.VMEM) for a in args]
    sources = [pltpu.with_memory_space_constraint(a, pltpu.HBM) for a in sources]
    return pl.pallas_call(
        kernel,
        in_specs=[pl.BlockSpec(memory_space=pltpu.HBM)] * len(sources) + [INNER] * len(args),
        out_shape=out_shape,
        scratch_shapes=scratch_shapes,
        compiler_params=pltpu.CompilerParams(vmem_limit_bytes=limit << 20),
        name=name,
    )(*sources, *args)


def exchange(sends):
    halos = []
    for k, send in enumerate(sends):
        axis = AXES[k // 2]
        count = lax.axis_size(axis)
        move = 1 if k % 2 == 0 else -1
        halos.append(lax.ppermute(send, axis, [(i, (i + move) % count) for i in range(count)]))
    return halos


def shards(state, convection, inverse_mass, face_coupling, lower_bound, upper_bound, new_owner):
    state = state.reshape(ZONES, WIDTH)
    convection = convection.reshape(ZONES, DOFS * DOFS)
    inverse_mass = inverse_mass.reshape(ZONES, DOFS * DOFS)
    lower_bound = lower_bound.reshape(ZONES, WIDTH)
    upper_bound = upper_bound.reshape(ZONES, WIDTH)
    owner = new_owner.reshape(1, ZONES)
    devices = lax.axis_size(AXES)
    pick, expand, order, rows, columns = [
        jnp.asarray(t, BF16) for t in (pick_table(), expand_table(), order_table(), *coupling_tables())
    ]
    slots = pltpu.VMEM((1, ZONES), jnp.int32)
    table = pltpu.VMEM((WIDTH, 6 * FACE), BF16)
    sources = (state, pick, owner, face_coupling.T, rows, columns)
    state, work, payload, slot, spread, *sends = call(
        start_kernel,
        "begin",
        sources,
        (),
        [STATE, WORK, PAYLOAD, slots, table] + SEND_SHAPES,
        [pltpu.VMEM(a.shape, a.dtype) for a in sources] + [pltpu.SemaphoreType.DMA((len(sources),))],
        8,
    )
    for step in range(STEPS):
        halos = exchange(sends)
        pushed = call(push_kernel, "push", (convection, expand), (work,), STATE, APPLY_SCRATCH, 16)
        sources = (inverse_mass, lower_bound, upper_bound, expand)
        fields = (state, pushed, payload, spread, *halos)
        if step < STEPS - 1:
            state, work, payload, *sends = call(
                step_kernel,
                "step_on",
                (*sources, pick),
                fields,
                [STATE, WORK, PAYLOAD] + SEND_SHAPES,
                [*UPDATE_SCRATCH, pltpu.VMEM(pick.shape, BF16)],
                24,
            )
    outgoing = call(
        last_kernel,
        "finish",
        (*sources, order),
        (*fields, slot),
        jax.ShapeDtypeStruct((devices * CAP, WIDTH), BF16),
        [STATE, *UPDATE_SCRATCH, pltpu.VMEM(order.shape, BF16)],
        24,
    )
    arrived = lax.all_to_all(outgoing.reshape(devices, CAP, WIDTH), AXES, split_axis=0, concat_axis=0, tiled=True)
    return arrived.reshape(devices * CAP, WIDTH).astype(F32)


def solution(mesh):
    in_specs = (
        P("gx", "gy", "gz", None),
        P("gx", "gy", "gz", None),
        P("gx", "gy", "gz", None),
        P(),
        P("gx", "gy", "gz", None),
        P("gx", "gy", "gz", None),
        P(AXES, None, None),
    )
    out_specs = P(AXES, None)
    return jax.shard_map(shards, mesh=mesh, in_specs=in_specs, out_specs=out_specs, check_vma=False)
```

```python
import jax
import jax.numpy as jnp
import numpy as np
from jax import lax
from jax.experimental import pallas as pl
from jax.experimental.pallas import tpu as pltpu
from jax.sharding import PartitionSpec as P

COMP = 4
DOFS = 64
STEPS = 2
WIDTH = COMP * DOFS
EX, EY, EZ = 4, 8, 32
ZONES = EX * EY * EZ
PLANE = EY * EZ
TILE = 128
TILES = ZONES // TILE
GROUP = 16
FACE = COMP * 16
CAP = 16
AXES = ("gx", "gy", "gz")
F32 = jnp.float32
BF16 = jnp.bfloat16
ORDER = np.arange(WIDTH).reshape(COMP, DOFS // 2, 2).transpose(1, 0, 2).reshape(WIDTH)


def pick_table():
    table = np.zeros((6, COMP, 16, COMP, 4, 4, 4), np.float32)
    for c in range(COMP):
        for f in range(16):
            p, q = f // 4, f % 4
            for side, level in ((0, 3), (1, 0)):
                table[0 + side, c, f, c, level, p, q] = 1
                table[2 + side, c, f, c, p, level, q] = 1
                table[4 + side, c, f, c, p, q, level] = 1
    return table.reshape(6 * FACE, WIDTH)[:, ORDER]


def expand_table():
    table = np.zeros((COMP, DOFS, WIDTH * 2), np.float32)
    for n, c in enumerate((0, 1, 2, 3, 1, 0, 3, 2)):
        table[c, :, DOFS * n : DOFS * (n + 1)] = np.eye(DOFS)
    return table.reshape(WIDTH, 2 * WIDTH)[ORDER]


def coupling_tables():
    rows = np.tile(np.eye(DOFS, dtype=np.float32), (COMP, 1))[ORDER]
    columns = np.zeros((6, 16, 6, COMP, 16), np.float32)
    for k in range(6):
        for f in range(16):
            columns[k, f, k, :, f] = 1
    return rows, columns.reshape(96, 6 * FACE)


def order_table():
    return np.eye(WIDTH, dtype=np.float32)[:, ORDER]


def dot(a, b):
    return jnp.dot(a, b, preferred_element_type=F32)


def select_zones(zone_of, count):
    column = lax.broadcasted_iota(jnp.int32, (1, 128), 1)
    wanted = jnp.where(column < count, zone_of(column), -1)
    zone = lax.broadcasted_iota(jnp.int32, (ZONES, 128), 0)
    return jnp.where(zone == wanted, 1.0, 0.0).astype(BF16)


def place_zones(zone_of, count):
    row = lax.broadcasted_iota(jnp.int32, (128, 1), 0)
    wanted = jnp.where(row < count, zone_of(row), -1)
    zone = lax.broadcasted_iota(jnp.int32, (128, ZONES), 1)
    return jnp.where(zone == wanted, 1.0, 0.0).astype(BF16)


def y_zone(level):
    return lambda n: (n // EZ) * PLANE + level * EZ + n % EZ


def z_zone(level):
    return lambda n: n * EZ + level


SENDS = ((64, 256), (64, 256), (64, 128), (64, 128), (64, 128), (64, 128))


def write_faces(work, pick, payload_ref, send_refs):
    payload = dot(pick, work).astype(BF16)
    payload_ref[...] = payload

    def face(k):
        return payload[FACE * k : FACE * (k + 1)]

    pieces = (
        face(0)[:, ZONES - PLANE :].astype(F32),
        face(1)[:, :PLANE].astype(F32),
        dot(face(2), select_zones(y_zone(EY - 1), EX * EZ)),
        dot(face(3), select_zones(y_zone(0), EX * EZ)),
        dot(face(4), select_zones(z_zone(EZ - 1), EX * EY)),
        dot(face(5), select_zones(z_zone(0), EX * EY)),
    )
    for k in range(6):
        index = lax.axis_index(AXES[k // 2])
        inner = index > 0 if k % 2 else index < lax.axis_size(AXES[k // 2]) - 1
        send_refs[k][...] = jnp.where(inner, pieces[k], 0.0).astype(BF16)


def incoming_flux(payload_ref, halo_refs, spread_ref, incoming_ref):
    def face(k):
        return payload_ref[FACE * k : FACE * (k + 1), :]

    incoming_ref[0:FACE, 0:PLANE] = halo_refs[0][...]
    incoming_ref[0:FACE, PLANE:ZONES] = payload_ref[0:FACE, 0 : ZONES - PLANE]
    incoming_ref[FACE : 2 * FACE, 0 : ZONES - PLANE] = payload_ref[FACE : 2 * FACE, PLANE:ZONES]
    incoming_ref[FACE : 2 * FACE, ZONES - PLANE : ZONES] = halo_refs[1][...]
    zone = lax.broadcasted_iota(jnp.int32, (FACE, ZONES), 1)
    third = zone % EZ
    second = zone // EZ % EY
    cases = (
        (2, EZ, second == 0, y_zone(0), EX * EZ),
        (3, ZONES - EZ, second == EY - 1, y_zone(EY - 1), EX * EZ),
        (4, 1, third == 0, z_zone(0), EX * EY),
        (5, ZONES - 1, third == EZ - 1, z_zone(EZ - 1), EX * EY),
    )
    for k, shift, edge, zone_of, count in cases:
        moved = pltpu.roll(face(k).astype(F32), shift, 1)
        placed = dot(halo_refs[k][...], place_zones(zone_of, count))
        incoming_ref[FACE * k : FACE * (k + 1), :] = jnp.where(edge, placed, moved).astype(BF16)
    return dot(spread_ref[...], incoming_ref[...])


def swap_blocks(parts, axis, block):
    size = parts[0].shape[axis]
    place = lax.broadcasted_iota(jnp.int32, parts[0].shape, axis) // block
    parts = list(parts)
    half = len(parts) // 2
    while half:
        low = (place & half) == 0
        for v in range(len(parts)):
            if v & half == 0:
                a, b = parts[v], parts[v + half]
                parts[v] = jnp.where(low, a, pltpu.roll(b, half * block, axis))
                parts[v + half] = jnp.where(low, pltpu.roll(a, size - half * block, axis), b)
        half //= 2
    return parts


def turned(rows):
    columns = rows.T
    parts = []
    for k in range(DOFS // 8):
        parts += swap_blocks([columns[DOFS * c + 8 * k : DOFS * c + 8 * k + 8] for c in range(COMP)], 0, 2)
    return parts


def tile(t):
    return pl.ds(pl.multiple_of(t * TILE, TILE), TILE)


def fetches(pairs, sems, first=0):
    return [pltpu.make_async_copy(source, target, sems.at[first + n]) for n, (source, target) in enumerate(pairs)]


def fetch_tile(source_ref, target_ref, sems, t):
    return pltpu.make_async_copy(source_ref.at[tile(t)], target_ref.at[tile(t)], sems.at[t])


def apply_matrices(wait, prepare, matrix_ref, values_ref, expand_ref, left_refs, product_refs, emit):
    zone = lax.broadcasted_iota(jnp.int32, (8, TILE), 1) % GROUP
    odds = [zone & bit != 0 for bit in (1, 2, 4, 8)]
    shape = (8 * GROUP, TILE)
    half = lax.broadcasted_iota(jnp.int32, shape, 0) % 2 == lax.broadcasted_iota(jnp.int32, shape, 1) // DOFS

    def expand(t, left_ref):
        expanded = lax.dot_general(
            values_ref[:, tile(t)], expand_ref[...], (((0,), (0,)), ((), ())), preferred_element_type=F32
        )
        for n in range(8):
            c, s = n // 2, n % 2
            source = c // 2 + (0 if c % 2 == s else 2)
            left_ref[pl.ds(n, TILE, stride=8), :] = expanded[:, TILE * source : TILE * (source + 1)]

    def multiply(t, left_ref, product_ref):
        for g in range(TILE // GROUP):
            left = jnp.where(half, left_ref[8 * GROUP * g : 8 * GROUP * (g + 1), :], 0.0).astype(BF16)
            matrix = matrix_ref[pl.ds(pl.multiple_of(t * TILE + GROUP * g, GROUP), GROUP), :]
            right = jnp.concatenate([matrix[:, TILE * m : TILE * (m + 1)] for m in range(DOFS // 2)], axis=0)
            product = lax.dot_general(left, right, (((1,), (1,)), ((), ())), preferred_element_type=F32)
            for q in range(4):
                lanes = slice(TILE * q, TILE * (q + 1))
                kept = [product[8 * z : 8 * z + 8, lanes] for z in range(GROUP)]
                for odd in odds:
                    kept = [jnp.where(odd, b, a) for a, b in zip(kept[0::2], kept[1::2])]
                product_ref[8 * g : 8 * g + 8, lanes] = kept[0]

    def settle(t, slot):
        product_ref = product_refs[slot]
        for q in range(4):
            parts = [product_ref[8 * g : 8 * g + 8, TILE * q : TILE * (q + 1)] for g in range(TILE // GROUP)]
            for n, part in enumerate(swap_blocks(parts, 1, GROUP)):
                emit(t, slot, 8 * q + n, part)

    (even_left, odd_left), (even_product, odd_product) = left_refs, product_refs
    expand(0, even_left)
    odd_product[...] = jnp.zeros_like(odd_product)

    def pair(n, carry):
        t = 2 * n
        wait(t)
        wait(t + 1)
        settle(jnp.maximum(t - 1, 0), 1)
        prepare(t, 0)
        expand(t + 1, odd_left)
        multiply(t, even_left, even_product)
        settle(t, 0)
        prepare(t + 1, 1)
        expand(jnp.minimum(t + 2, TILES - 1), even_left)
        multiply(t + 1, odd_left, odd_product)
        return carry

    lax.fori_loop(0, TILES // 2, pair, 0)
    settle(TILES - 1, 1)


def start_kernel(*refs):
    sources, (u_ref, work_ref, payload_ref, slot_ref, spread_ref), send_refs = refs[:6], refs[6:11], refs[11:17]
    targets, sems = refs[17:23], refs[23]
    state_ref, pick_ref, owner_ref, coupling_ref, rows_ref, columns_ref = targets
    copies = fetches(list(zip(sources, targets)), sems)
    for copy in copies[::-1]:
        copy.start()
    for copy in copies[2:]:
        copy.wait()
    before = lax.broadcasted_iota(jnp.int32, (TILE, TILE), 0) < lax.broadcasted_iota(jnp.int32, (TILE, TILE), 1)
    before = jnp.where(before, 1.0, 0.0).astype(BF16)
    owners = lax.broadcasted_iota(jnp.int32, (128, TILE), 0)
    carry = jnp.zeros((128, 1), F32)
    for t in range(TILES):
        owner = owner_ref[:, TILE * t : TILE * (t + 1)]
        match = jnp.where(owners == owner, 1.0, 0.0)
        earlier = dot(match.astype(BF16), before) + carry
        rank = jnp.sum(earlier * match, axis=0, keepdims=True)
        slot_ref[:, TILE * t : TILE * (t + 1)] = owner * CAP + rank.astype(jnp.int32)
        carry = carry + jnp.sum(match, axis=1, keepdims=True)
    entries = dot(rows_ref[...], coupling_ref[...])
    entries = dot(entries.astype(BF16), columns_ref[...])
    own = lax.broadcasted_iota(jnp.int32, entries.shape, 0) // 2 % COMP
    theirs = lax.broadcasted_iota(jnp.int32, entries.shape, 1) // 16 % COMP
    spread_ref[...] = jnp.where(own == theirs, entries, 0.0).astype(BF16)
    copies[0].wait()
    for t in range(TILES):
        lanes = slice(TILE * t, TILE * (t + 1))
        for m, part in enumerate(turned(state_ref[lanes, :])):
            u_ref[8 * m : 8 * m + 8, lanes] = part
    work = u_ref[...].astype(BF16)
    work_ref[...] = work
    copies[1].wait()
    write_faces(work, pick_ref[...], payload_ref, send_refs)


def push_kernel(matrix_source, expand_source, work_ref, pushed_ref, *scratch):
    left_refs, product_refs, (matrix_ref, expand_ref, sems) = scratch[0:2], scratch[2:4], scratch[4:7]
    (expanded,) = fetches([(expand_source, expand_ref)], sems, TILES)
    expanded.start()
    for t in range(TILES):
        fetch_tile(matrix_source, matrix_ref, sems, t).start()
    expanded.wait()

    def emit(t, slot, m, part):
        pushed_ref[8 * m : 8 * m + 8, tile(t)] = part

    def wait(t):
        fetch_tile(matrix_source, matrix_ref, sems, t).wait()

    apply_matrices(wait, lambda t, slot: None, matrix_ref, work_ref, expand_ref, left_refs, product_refs, emit)


def update(sources, fields, halo_refs, next_ref, scratch):
    u_ref, pushed_ref, payload_ref, spread_ref = fields
    (incoming_ref, rhs_ref), left_refs, product_refs = scratch[0:2], scratch[2:4], scratch[4:6]
    (matrix_ref, expand_ref, sems), lower_refs, upper_refs = scratch[6:9], scratch[9:11], scratch[11:13]
    low_ref, high_ref, table_ref = scratch[13:]
    expanded, low, high, table = fetches(
        [(sources[3], expand_ref), (sources[1], low_ref), (sources[2], high_ref), (sources[4], table_ref)], sems, TILES
    )
    for copy in (expanded, low, high):
        copy.start()
    for t in range(TILES):
        fetch_tile(sources[0], matrix_ref, sems, t).start()
    table.start()
    rhs_ref[...] = (pushed_ref[...] + incoming_flux(payload_ref, halo_refs, spread_ref, incoming_ref)).astype(BF16)
    low.wait()
    high.wait()
    expanded.wait()

    def prepare(t, slot):
        for m, part in enumerate(turned(low_ref[tile(t), :])):
            lower_refs[slot][8 * m : 8 * m + 8, :] = part
        for m, part in enumerate(turned(high_ref[tile(t), :])):
            upper_refs[slot][8 * m : 8 * m + 8, :] = part

    def emit(t, slot, m, part):
        rows = slice(8 * m, 8 * m + 8)
        moved = u_ref[rows, tile(t)] + part
        next_ref[rows, tile(t)] = jnp.minimum(jnp.maximum(moved, lower_refs[slot][rows, :]), upper_refs[slot][rows, :])

    def wait(t):
        fetch_tile(sources[0], matrix_ref, sems, t).wait()

    apply_matrices(wait, prepare, matrix_ref, rhs_ref, expand_ref, left_refs, product_refs, emit)
    table.wait()
    return table_ref[...]


def step_kernel(*refs):
    sources, fields, halo_refs, refs = refs[:5], refs[5:9], refs[9:15], refs[15:]
    (next_ref, work_ref, next_payload_ref), send_refs, scratch = refs[:3], refs[3:9], refs[9:]
    pick = update(sources, fields, halo_refs, next_ref, scratch)
    work = next_ref[...].astype(BF16)
    work_ref[...] = work
    write_faces(work, pick, next_payload_ref, send_refs)


def last_kernel(*refs):
    sources, fields, halo_refs, slot_ref, refs = refs[:5], refs[5:9], refs[9:15], refs[15], refs[16:]
    outgoing_ref, next_ref, scratch = refs[0], refs[1], refs[2:]
    order = update(sources, fields, halo_refs, next_ref, scratch)
    chunk = 512
    slot = slot_ref[...]
    work = dot(order, next_ref[...].astype(BF16)).astype(BF16)

    def place(n, carry):
        first = pl.multiple_of(n * chunk, chunk)
        rows = lax.broadcasted_iota(jnp.int32, (chunk, ZONES), 0) + first
        match = jnp.where(rows == slot, 1.0, 0.0).astype(BF16)
        taken = lax.dot_general(match, work, (((1,), (1,)), ((), ())), preferred_element_type=F32)
        outgoing_ref[pl.ds(first, chunk), :] = taken.astype(BF16)
        return carry

    lax.fori_loop(0, outgoing_ref.shape[0] // chunk, place, 0)


INNER = pl.BlockSpec(memory_space=pltpu.VMEM)
SEND_SHAPES = [pltpu.VMEM(s, BF16) for s in SENDS]
STATE = pltpu.VMEM((WIDTH, ZONES), F32)
WORK = pltpu.VMEM((WIDTH, ZONES), BF16)
PAYLOAD = pltpu.VMEM((6 * FACE, ZONES), BF16)
APPLY_SCRATCH = [
    *[pltpu.VMEM((8 * TILE, TILE), F32)] * 2,
    *[pltpu.VMEM((TILE // GROUP * 8, DOFS // 2 * GROUP), F32)] * 2,
    pltpu.VMEM((ZONES, DOFS * DOFS), BF16),
    pltpu.VMEM((WIDTH, 2 * WIDTH), BF16),
    pltpu.SemaphoreType.DMA((TILES + 4,)),
]
ROWMAJOR = pltpu.VMEM((ZONES, WIDTH), F32)
UPDATE_SCRATCH = [PAYLOAD, WORK, *APPLY_SCRATCH, *[pltpu.VMEM((WIDTH, TILE), F32)] * 4, ROWMAJOR, ROWMAJOR]


def call(kernel, name, sources, args, out_shape, scratch_shapes, limit):
    args = [pltpu.with_memory_space_constraint(a, pltpu.VMEM) for a in args]
    sources = [pltpu.with_memory_space_constraint(a, pltpu.HBM) for a in sources]
    return pl.pallas_call(
        kernel,
        in_specs=[pl.BlockSpec(memory_space=pltpu.HBM)] * len(sources) + [INNER] * len(args),
        out_shape=out_shape,
        scratch_shapes=scratch_shapes,
        compiler_params=pltpu.CompilerParams(vmem_limit_bytes=limit << 20),
        name=name,
    )(*sources, *args)


def exchange(sends):
    halos = []
    for k, send in enumerate(sends):
        axis = AXES[k // 2]
        count = lax.axis_size(axis)
        move = 1 if k % 2 == 0 else -1
        halos.append(lax.ppermute(send, axis, [(i, (i + move) % count) for i in range(count)]))
    return halos


def shards(state, convection, inverse_mass, face_coupling, lower_bound, upper_bound, new_owner):
    state = state.reshape(ZONES, WIDTH)
    convection = convection.reshape(ZONES, DOFS * DOFS)
    inverse_mass = inverse_mass.reshape(ZONES, DOFS * DOFS)
    lower_bound = lower_bound.reshape(ZONES, WIDTH)
    upper_bound = upper_bound.reshape(ZONES, WIDTH)
    owner = new_owner.reshape(1, ZONES)
    devices = lax.axis_size(AXES)
    pick, expand, order, rows, columns = [
        jnp.asarray(t, BF16) for t in (pick_table(), expand_table(), order_table(), *coupling_tables())
    ]
    slots = pltpu.VMEM((1, ZONES), jnp.int32)
    table = pltpu.VMEM((WIDTH, 6 * FACE), BF16)
    sources = (state, pick, owner, face_coupling.T, rows, columns)
    state, work, payload, slot, spread, *sends = call(
        start_kernel,
        "begin",
        sources,
        (),
        [STATE, WORK, PAYLOAD, slots, table] + SEND_SHAPES,
        [pltpu.VMEM(a.shape, a.dtype) for a in sources] + [pltpu.SemaphoreType.DMA((len(sources),))],
        8,
    )
    for step in range(STEPS):
        halos = exchange(sends)
        pushed = call(push_kernel, "push", (convection, expand), (work,), STATE, APPLY_SCRATCH, 16)
        sources = (inverse_mass, lower_bound, upper_bound, expand)
        fields = (state, pushed, payload, spread, *halos)
        if step < STEPS - 1:
            state, work, payload, *sends = call(
                step_kernel,
                "step_on",
                (*sources, pick),
                fields,
                [STATE, WORK, PAYLOAD] + SEND_SHAPES,
                [*UPDATE_SCRATCH, pltpu.VMEM(pick.shape, BF16)],
                24,
            )
    outgoing = call(
        last_kernel,
        "finish",
        (*sources, order),
        (*fields, slot),
        jax.ShapeDtypeStruct((devices * CAP, WIDTH), BF16),
        [STATE, *UPDATE_SCRATCH, pltpu.VMEM(order.shape, BF16)],
        24,
    )
    arrived = lax.all_to_all(outgoing.reshape(devices, CAP, WIDTH), AXES, split_axis=0, concat_axis=0, tiled=True)
    return arrived.reshape(devices * CAP, WIDTH).astype(F32)


def solution(mesh):
    in_specs = (
        P("gx", "gy", "gz", None),
        P("gx", "gy", "gz", None),
        P("gx", "gy", "gz", None),
        P(),
        P("gx", "gy", "gz", None),
        P("gx", "gy", "gz", None),
        P(AXES, None, None),
    )
    out_specs = P(AXES, None)
    return jax.shard_map(shards, mesh=mesh, in_specs=in_specs, out_specs=out_specs, check_vma=False)
```
